512 devices in a mesh: dp: 32 (over y_hi, x, core), tensor: 16 (over z, y_lo).
Axes of the slice: x: 4, y: 8 (y_hi: 4, y_lo: 2; y = y_hi * 2 + y_lo), z: 8, core: 2. Of those that a mesh axis runs over, the one named last changes fastest.
Arguments:
- tokens: bfloat16 [12288, 2048], P('dp'), may hold values from -6 to 6
- out_grad: bfloat16 [12288, 7168], P('dp', 'tensor'), may hold values from -6 to 6
- gate_weight: bfloat16 [2048, 7168], P('dp', 'tensor'), may hold values from -0.1875 to 0.1875
- up_weight: bfloat16 [2048, 7168], P('dp', 'tensor'), may hold values from -0.1875 to 0.1875
- gate_mask: int32 [32, 112], P('dp', 'tensor'), may hold values 0 or 1
- up_mask: int32 [32, 112], P('dp', 'tensor'), may hold values 0 or 1
Outputs:
- hidden: float32 [12288, 7168], P('dp', 'tensor')
- grad_tokens: bfloat16 [12288, 2048], P('dp')
- grad_gate: float32 [2048, 7168], P('dp', 'tensor')
- grad_up: float32 [2048, 7168], P('dp', 'tensor')
The draws below stay inside these ranges and needn't reach their ends.
All inputs are finite; a program needn't handle non-finite values. No bound on the sum of `gate_mask` or of `up_mask` on one device may be relied on, other than what follows from the above.
Results may differ from the reference program's by a relative error of at most 0.014.
Values may be sent and summed in bfloat16 or wider, within the bound.
No kernel may reach another device: no remote copies, remote signals or barrier semaphores. Data moves between devices by JAX's collectives and lax.ppermute only.
A program may use at most 64 MiB of HBM per device.

```python
import jax
import jax.numpy as jnp
from jax import lax

D = 2048
FF = 7168
BLOCK = 64
TOK_GROUP = 384
TOKENS = 12288
N_DP = 32


def touch_ends(drawn, rng, least, high):
    spot = [jax.random.randint(jax.random.fold_in(rng, axis), (), 0, length) for axis, length in enumerate(drawn.shape)]
    longest = drawn.shape.index(max(drawn.shape))
    beside = spot[:longest] + [(spot[longest] + 1) % drawn.shape[longest]] + spot[longest + 1:]
    return drawn.at[tuple(spot)].set(least).at[tuple(beside)].set(high)


def with_spikes(array, own_key, source, target, blocks, factor):
    def block_of(axis_at):
        return (jnp.arange(array.shape[axis_at]) // (array.shape[axis_at] // blocks)).reshape((-1,) + (1,) * (array.ndim - 1 - axis_at))

    near = jax.random.permutation(own_key, blocks)[block_of(target)]
    other_side = (block_of(target) + blocks // 2) % blocks
    return jnp.where((block_of(source) == near) | (block_of(source) == other_side), factor * array, array)


def shard_levels(key, dims, cuts, low, top_value):
    level = 1.0
    for position, parts in cuts:
        steps = jax.random.uniform(jax.random.fold_in(jax.random.fold_in(key, 6), position), (parts,), jnp.float32, low / len(cuts), top_value / len(cuts))
        level = level * jnp.repeat(jnp.exp(steps), dims[position] // parts).reshape((-1,) + (1,) * (len(dims) - 1 - position))
    return level


def bell_draw(own_key, extent, deviation, most, cuts=(), held_as=jnp.bfloat16):
    level = shard_levels(own_key, extent, cuts, -0.22, 0.18) if cuts else 1.0
    result = jax.random.normal(own_key, extent, jnp.float32) * deviation * level
    return jnp.minimum(jnp.maximum(result, -most), most).astype(held_as)


def noise_with(own_key, dims, deviation, most, split, heavy, dtype=jnp.bfloat16):
    entries = deviation * jax.random.normal(own_key, dims, jnp.float32)
    if split:
        entries = entries * shard_levels(own_key, dims, split, -0.22, 0.18)
    return jnp.clip(with_spikes(entries, jax.random.fold_in(own_key, 3), *heavy), -most, most).astype(dtype)


def setup_inputs(seed: int = 0) -> dict:
    arg_keys = jax.random.split(jax.random.key(seed), 7)
    tokens = noise_with(arg_keys[0], (TOKENS, D), 1.0, 6.0, ((0, 32),), (0, 1, 32, 2.75))
    out_grad = bell_draw(arg_keys[1], (TOKENS, FF), 1.0, 6.0, ((0, 32), (1, 16)))
    gate_weight = bell_draw(arg_keys[2], (D, FF), (D // 2) ** -0.5, 0.1875, ((0, 32), (1, 16)))
    up_weight = bell_draw(arg_keys[3], (D, FF), (D // 2) ** -0.5, 0.1875, ((0, 32), (1, 16)))
    gate_mask = touch_ends((jax.random.randint(arg_keys[4], (D // BLOCK, FF // BLOCK), 0, 2) < 1).astype(jnp.int32), jax.random.fold_in(arg_keys[4], 1), 0, 1)
    up_mask = touch_ends((jax.random.randint(arg_keys[5], (D // BLOCK, FF // BLOCK), 0, 2) < 1).astype(jnp.int32), jax.random.fold_in(arg_keys[5], 1), 0, 1)
    return {"tokens": tokens, "out_grad": out_grad, "gate_weight": gate_weight, "up_weight": up_weight, "gate_mask": gate_mask, "up_mask": up_mask}


def expand(block_mask):
    height, breadth = block_mask.shape
    values = block_mask.astype(jnp.float32)
    return jnp.broadcast_to(values[:, None, :, None], (height, BLOCK, breadth, BLOCK)).reshape(height * BLOCK, breadth * BLOCK)


def reference(tokens, out_grad, gate_weight, up_weight, gate_mask, up_mask):
    gate_keep = expand(gate_mask)
    up_keep = expand(up_mask)
    gate_eff = (gate_weight.astype(jnp.float32) * gate_keep).astype(jnp.bfloat16)
    up_eff = (up_weight.astype(jnp.float32) * up_keep).astype(jnp.bfloat16)
    both_eff = jnp.concatenate([gate_eff, up_eff], axis=1)
    token_groups = tokens.reshape(N_DP, TOK_GROUP, D)
    grad_groups = out_grad.reshape(N_DP, TOK_GROUP, FF)

    def group_step(grad_total, operands):
        group_tokens, group_grad = operands
        preact = jnp.dot(group_tokens, both_eff, preferred_element_type=jnp.float32)
        gate = preact[:, :FF]
        up = preact[:, FF:]
        sigmoid_gate = jax.nn.sigmoid(gate)
        activation = gate * sigmoid_gate
        hidden = activation * up
        grad_float = group_grad.astype(jnp.float32)
        d_gate = (grad_float * up * sigmoid_gate * (1.0 + gate * (1.0 - sigmoid_gate))).astype(jnp.bfloat16)
        d_up = (grad_float * activation).astype(jnp.bfloat16)
        d_both = jnp.concatenate([d_gate, d_up], axis=1)
        input_grad = lax.dot_general(d_both, both_eff, (((1,), (1,)), ((), ())), preferred_element_type=jnp.float32).astype(jnp.bfloat16)
        partial_rows = lax.dot_general(group_tokens, d_both, (((0,), (0,)), ((), ())), preferred_element_type=jnp.float32).astype(jnp.bfloat16)
        partial_rows = lax.optimization_barrier(partial_rows)
        grad_total = grad_total + partial_rows.astype(jnp.float32)
        return grad_total, (hidden, input_grad)

    grad_total, (hidden_all, input_all) = lax.scan(group_step, jnp.zeros((D, 2 * FF), jnp.float32), (token_groups, grad_groups))
    grad_gate = grad_total[:, :FF] * gate_keep
    grad_up = grad_total[:, FF:] * up_keep
    return hidden_all.reshape(TOKENS, FF), input_all.reshape(TOKENS, D), grad_gate, grad_up
```

```python
import jax
import jax.numpy as jnp
import numpy as np
from jax import lax
from jax.experimental import pallas as pl
from jax.experimental.pallas import tpu as pltpu
from jax.sharding import Mesh
from jax.sharding import PartitionSpec as P

BLOCK = 64
BF16 = jnp.bfloat16
F32 = jnp.float32
YH, X, CORE, Z, YL = 4, 4, 2, 8, 2
VM = pl.BlockSpec(memory_space=pltpu.VMEM)
SM = pl.BlockSpec(memory_space=pltpu.SMEM)


def keep_row(mask_ref, width):
    column = lax.broadcasted_iota(jnp.int32, (1, width), 1) // BLOCK
    keep = jnp.zeros((1, width), F32)
    for block in range(width // BLOCK):
        keep = jnp.where(column == block, mask_ref[0, block].astype(F32), keep)
    return keep


def mask_kernel(gm, um, gw, uw, out):
    width = gw.shape[1]
    gate = gw[...].astype(F32) * keep_row(gm, width)
    up = uw[...].astype(F32) * keep_row(um, width)
    both = jnp.concatenate([gate, up], axis=1).astype(BF16)
    for copy in range(YH):
        out[copy] = both


def forward_kernel(place, tokens, ogt, mine, other, hidden_t, d_both, send, keep, w):
    core = place[0]
    half = place[1]
    width = ogt.shape[0]
    for yh in range(YH):
        for x in range(X):
            w[yh * X + x, core] = mine[x, yh]
            w[yh * X + x, 1 - core] = other[x, yh]
    weights = w[...].reshape(YH * X * CORE * BLOCK, 2 * width)
    preact = jnp.dot(tokens[...], weights, preferred_element_type=F32)
    gate = preact[:, :width]
    up = preact[:, width:]
    sigmoid = jax.nn.sigmoid(gate)
    activation = gate * sigmoid
    hidden_t[...] = (activation * up).T
    grad = ogt[...].astype(F32).T
    d_gate = grad * up * sigmoid * (1.0 + gate * (1.0 - sigmoid))
    d_up = grad * activation
    d_both[...] = jnp.concatenate([d_gate, d_up], axis=1).astype(BF16)
    rows = send.shape[0]

    def partial(index):
        part = d_both[pl.ds(pl.multiple_of(index * rows, rows), rows), :]
        return lax.dot_general(
            part, weights, (((1,), (1,)), ((), ())), preferred_element_type=F32
        ).astype(BF16)

    send[...] = partial(1 - half)
    keep[...] = partial(half)


def weight_kernel(place, tokens, d_both, keep, send):
    core = place[0]
    rows = CORE * BLOCK * 2
    for step in range(YH * X // 2):
        both = lax.dot_general(
            tokens[:, step * rows : (step + 1) * rows],
            d_both[...],
            (((0,), (0,)), ((), ())),
            preferred_element_type=F32,
        ).astype(BF16)
        for pair in range(2):
            yh, x = divmod(step * 2 + pair, X)
            low = both[pair * 128 : pair * 128 + 64]
            high = both[pair * 128 + 64 : pair * 128 + 128]
            first = core == 0
            keep[x, yh] = jnp.where(first, low, high)
            send[x, yh] = jnp.where(first, high, low)


def final_kernel(gm, um, parts, grad_gate, grad_up):
    width = grad_gate.shape[1]
    total = parts[0].astype(F32)
    for source in range(1, YH):
        total = total + parts[source].astype(F32)
    grad_gate[...] = total[:, :width] * keep_row(gm, width)
    grad_up[...] = total[:, width:] * keep_row(um, width)


def shape(dims, dtype=BF16):
    return jax.ShapeDtypeStruct(dims, dtype)


def params():
    return pltpu.CompilerParams(vmem_limit_bytes=40 << 20)


def swap(array, axis):
    return lax.ppermute(array, axis, [(0, 1), (1, 0)])


def local(tokens, out_grad, gate_weight, up_weight, gate_mask, up_mask):
    width = gate_weight.shape[1]
    count, features = tokens.shape
    half = count // YL
    chunk = half // Z
    place = jnp.stack([lax.axis_index("core"), lax.axis_index("yl")]).astype(jnp.int32)
    with jax.named_scope("mask"):
        copies = pl.pallas_call(
            mask_kernel,
            in_specs=[SM, SM, VM, VM],
            out_specs=VM,
            out_shape=shape((YH, BLOCK, 2 * width)),
        )(gate_mask, up_mask, gate_weight, up_weight)
    with jax.named_scope("gather_yh"):
        rows = lax.all_to_all(copies, "yh", 0, 0, tiled=True)
    with jax.named_scope("gather_x"):
        rows = jnp.broadcast_to(rows[None], (X,) + rows.shape)
        mine = lax.all_to_all(rows, "x", 0, 0, tiled=True)
    with jax.named_scope("gather_core"):
        other = swap(mine, "core")
    with jax.named_scope("forward"):
        hidden_t, d_both, send, keep = pl.pallas_call(
            forward_kernel,
            in_specs=[SM, VM, VM, VM, VM],
            out_specs=[VM] * 4,
            out_shape=[
                shape((width, count), F32),
                shape((count, 2 * width)),
                shape((half, features)),
                shape((half, features)),
            ],
            scratch_shapes=[pltpu.VMEM((YH * X, CORE, BLOCK, 2 * width), BF16)],
            compiler_params=params(),
        )(place, tokens, out_grad.T, mine, other)
    with jax.named_scope("tensor_yl"):
        received = swap(send, "yl")
    with jax.named_scope("weights"):
        w_keep, w_send = pl.pallas_call(
            weight_kernel,
            in_specs=[SM, VM, VM],
            out_specs=[VM] * 2,
            out_shape=[shape((X, YH, BLOCK, 2 * width))] * 2,
            compiler_params=params(),
        )(place, tokens, d_both)
    with jax.named_scope("scatter_core"):
        w_received = swap(w_send, "core")
    w_sum = (w_keep.astype(F32) + w_received.astype(F32)).astype(BF16)
    x_sum = (keep.astype(F32) + received.astype(F32)).astype(BF16)
    with jax.named_scope("scatter_x"):
        w_parts = lax.all_to_all(w_sum, "x", 0, 0, tiled=True)
    with jax.named_scope("tensor_z"):
        x_parts = lax.all_to_all(x_sum.reshape(Z, chunk, features), "z", 0, 0, tiled=True)
    w_sum = w_parts.astype(F32).sum(axis=0).astype(BF16)
    x_own = x_parts.astype(F32).sum(axis=0).astype(BF16)
    with jax.named_scope("scatter_yh"):
        w_parts = lax.all_to_all(w_sum, "yh", 0, 0, tiled=True)
    with jax.named_scope("tensor_back_z"):
        x_own = jnp.broadcast_to(x_own[None], (Z, chunk, features))
        x_half = lax.all_to_all(x_own, "z", 0, 0, tiled=True).reshape(half, features)
    with jax.named_scope("tensor_back_yl"):
        x_other = swap(x_half, "yl")
    with jax.named_scope("final"):
        grad_gate, grad_up = pl.pallas_call(
            final_kernel,
            in_specs=[SM, SM, VM],
            out_specs=[VM] * 2,
            out_shape=[shape((BLOCK, width), F32)] * 2,
        )(gate_mask, up_mask, w_parts)
    first = place[1] == 0
    grad_tokens = jnp.concatenate(
        [jnp.where(first, x_half, x_other), jnp.where(first, x_other, x_half)], axis=0
    )
    return (hidden_t.T, grad_tokens, grad_gate, grad_up)


def solution(mesh):
    fine = Mesh(
        np.asarray(mesh.devices).reshape(YH, X, CORE, Z, YL), ("yh", "x", "core", "z", "yl")
    )
    dp = ("yh", "x", "core")
    tensor = ("z", "yl")
    both = P(dp, tensor)
    return jax.shard_map(
        local,
        mesh=fine,
        in_specs=(P(dp, None), both, both, both, both, both),
        out_specs=(both, P(dp, None), both, both),
        check_vma=False,
    )
```

```python
import jax
import jax.numpy as jnp
import numpy as np
from jax import lax
from jax.experimental import pallas as pl
from jax.experimental.pallas import tpu as pltpu
from jax.sharding import Mesh
from jax.sharding import PartitionSpec as P


BLOCK = 64
BF16 = jnp.bfloat16
F32 = jnp.float32
YH, X, CORE, Z, YL = 4, 4, 2, 8, 2
PIECES = 2
VM = pl.BlockSpec(memory_space=pltpu.VMEM)
SM = pl.BlockSpec(memory_space=pltpu.SMEM)


def keep_row(mask_ref, width):
    column = lax.broadcasted_iota(jnp.int32, (1, width), 1) // BLOCK
    keep = jnp.zeros((1, width), F32)
    for block in range(width // BLOCK):
        keep = jnp.where(column == block, mask_ref[0, block].astype(F32), keep)
    return keep


def mask_kernel(gm, um, gw, uw, out):
    width = gw.shape[1]
    gate = gw[...].astype(F32) * keep_row(gm, width)
    up = uw[...].astype(F32) * keep_row(um, width)
    both = jnp.concatenate([gate, up], axis=1).astype(BF16)
    for copy in range(YH):
        out[copy] = both


def forward_kernel(place, tokens, ogt, *rest):
    mine, other = rest[:X], rest[X : 2 * X]
    hidden_t, d_both, *rest = rest[2 * X :]
    sends, keeps, w = rest[:PIECES], rest[PIECES:-1], rest[-1]
    core, half, own_x = place[0], place[1], place[2]
    width = ogt.shape[0]
    for yh in range(YH):
        for back in range(X):
            x = lax.rem(own_x + (X - back), X)
            w[yh * X + x, core] = mine[back][yh]
            w[yh * X + x, 1 - core] = other[back][yh]
    weights = w[...].reshape(YH * X * CORE * BLOCK, 2 * width)
    preact = jnp.dot(tokens[...], weights, preferred_element_type=F32)
    gate = preact[:, :width]
    up = preact[:, width:]
    sigmoid = jax.nn.sigmoid(gate)
    activation = gate * sigmoid
    hidden_t[...] = (activation * up).T
    grad = ogt[...].astype(F32).T
    d_gate = grad * up * sigmoid * (1.0 + gate * (1.0 - sigmoid))
    d_up = grad * activation
    d_both[...] = jnp.concatenate([d_gate, d_up], axis=1).astype(BF16)
    rows, columns = sends[0].shape
    for index, outs in ((1 - half, sends), (half, keeps)):
        part = d_both[pl.ds(pl.multiple_of(index * rows, rows), rows), :]
        for piece, out in enumerate(outs):
            out[...] = lax.dot_general(
                part,
                weights[piece * columns : (piece + 1) * columns],
                (((1,), (1,)), ((), ())),
                preferred_element_type=F32,
            ).astype(BF16)


def weight_kernel(place, tokens, d_both, keep, send):
    core, own_x, own_yh = place[0], place[2], place[3]
    rows = CORE * BLOCK * 2
    for step in range(YH * X // 2):
        both = lax.dot_general(
            tokens[:, step * rows : (step + 1) * rows],
            d_both[...],
            (((0,), (0,)), ((), ())),
            preferred_element_type=F32,
        ).astype(BF16)
        for pair in range(2):
            yh, x = divmod(step * 2 + pair, X)
            ahead = lax.rem(x + X - own_x, X), lax.rem(yh + YH - own_yh, YH)
            low = both[pair * 128 : pair * 128 + 64]
            high = both[pair * 128 + 64 : pair * 128 + 128]
            first = core == 0
            keep[ahead] = jnp.where(first, low, high)
            send[ahead] = jnp.where(first, high, low)


def final_kernel(gm, um, *refs):
    parts, (grad_gate, grad_up) = refs[:-2], refs[-2:]
    width = grad_gate.shape[1]
    total = parts[0][...].astype(F32)
    for part in parts[1:]:
        total = total + part[...].astype(F32)
    grad_gate[...] = total[:, :width] * keep_row(gm, width)
    grad_up[...] = total[:, width:] * keep_row(um, width)


def pair_kernel(first, second, *outs):
    for index, out in enumerate(outs):
        out[...] = (first[index].astype(F32) + second[index].astype(F32)).astype(BF16)


def rows_kernel(*refs):
    parts, outs = refs[:X], refs[X:]
    for index, out in enumerate(outs):
        total = parts[0][index].astype(F32)
        for part in parts[1:]:
            total = total + part[index].astype(F32)
        out[...] = total.astype(BF16)


def add_kernel(first, second, out):
    out[...] = (first[...].astype(F32) + second[...].astype(F32)).astype(BF16)


def total_of(parts):
    total = parts[0].astype(F32)
    for source in range(1, parts.shape[0]):
        total = total + parts[source].astype(F32)
    return total.astype(BF16)


def sum_copies_kernel(parts, out):
    total = total_of(parts)
    for copy in range(out.shape[0]):
        out[copy] = total


def join_kernel(place, *refs):
    mine, other, out = refs[:PIECES], refs[PIECES:-1], refs[-1]
    half = place[1]
    rows, columns = mine[0].shape
    for piece in range(PIECES):
        span = slice(piece * columns, (piece + 1) * columns)
        out[pl.ds(pl.multiple_of(half * rows, rows), rows), span] = mine[piece][...]
        out[pl.ds(pl.multiple_of((1 - half) * rows, rows), rows), span] = other[piece][...]


def shape(dims, dtype=BF16):
    return jax.ShapeDtypeStruct(dims, dtype)


def params():
    return pltpu.CompilerParams(vmem_limit_bytes=40 << 20)


def swap(array, axis):
    return lax.ppermute(array, axis, [(0, 1), (1, 0)])


def shift(array, axis, size, steps):
    return lax.ppermute(array, axis, [(i, (i + steps) % size) for i in range(size)])


def call(kernel, out_shape, *operands, scalars=0, scratch=()):
    many = isinstance(out_shape, list)
    results = pl.pallas_call(
        kernel,
        in_specs=[SM] * scalars + [VM] * (len(operands) - scalars),
        out_specs=[VM] * len(out_shape) if many else VM,
        out_shape=out_shape,
        scratch_shapes=list(scratch),
        compiler_params=params(),
    )(*operands)
    return list(results) if many else results


def compute(tokens, out_grad, gate_weight, up_weight, gate_mask, up_mask):
    width = gate_weight.shape[1]
    count, features = tokens.shape
    half = count // YL
    chunk = half // Z
    columns = features // PIECES
    place = jnp.stack([lax.axis_index(name) for name in ("core", "yl", "x", "yh")])
    copies = call(
        mask_kernel,
        shape((YH, BLOCK, 2 * width)),
        gate_mask,
        up_mask,
        gate_weight,
        up_weight,
        scalars=2,
    )
    rows = lax.all_to_all(copies, "yh", 0, 0, tiled=True)
    mine, other = [rows], []
    for steps in range(1, X):
        mine.append(shift(rows, "x", X, steps))
    for steps in range(X):
        other.append(swap(mine[steps], "core"))
    hidden_t, d_both, *partials = call(
        forward_kernel,
        [shape((width, count), F32), shape((count, 2 * width))]
        + [shape((half, columns))] * (2 * PIECES),
        place,
        tokens,
        out_grad.T,
        *mine,
        *other,
        scalars=1,
        scratch=[pltpu.VMEM((YH * X, CORE, BLOCK, 2 * width), BF16)],
    )
    sends, keeps = partials[:PIECES], partials[PIECES:]
    received = []
    for piece in range(PIECES):
        received.append(swap(sends[piece], "yl"))
    w_keep, w_send = call(
        weight_kernel,
        [shape((X, YH, BLOCK, 2 * width))] * 2,
        place,
        tokens,
        d_both,
        scalars=1,
    )
    w_received = swap(w_send, "core")
    w_parts = call(
        pair_kernel, [shape((YH, BLOCK, 2 * width))] * X, w_keep, w_received
    )
    for steps in range(1, X):
        w_parts[steps] = shift(w_parts[steps], "x", X, steps)
    w_parts = call(rows_kernel, [shape((BLOCK, 2 * width))] * YH, *w_parts)
    for steps in range(1, YH):
        w_parts[steps] = shift(w_parts[steps], "yh", YH, steps)
    grad_gate, grad_up = call(
        final_kernel,
        [shape((BLOCK, width), F32)] * 2,
        gate_mask,
        up_mask,
        *w_parts,
        scalars=2,
    )
    own, others = [], []
    for piece in range(PIECES):
        x_sum = call(add_kernel, shape((half, columns)), keeps[piece], received[piece])
        x_parts = lax.all_to_all(x_sum.reshape(Z, chunk, columns), "z", 0, 0, tiled=True)
        x_copies = call(sum_copies_kernel, shape((Z, chunk, columns)), x_parts)
        x_half = lax.all_to_all(x_copies, "z", 0, 0, tiled=True).reshape(half, columns)
        own.append(x_half)
        others.append(swap(x_half, "yl"))
    grad_tokens = call(
        join_kernel, shape((count, features)), place, *own, *others, scalars=1
    )
    return (hidden_t.T, grad_tokens, grad_gate, grad_up)


def solution(mesh):
    fine = Mesh(
        np.asarray(mesh.devices).reshape(YH, X, CORE, Z, YL), ("yh", "x", "core", "z", "yl")
    )
    dp = ("yh", "x", "core")
    tensor = ("z", "yl")
    both = P(dp, tensor)
    return jax.shard_map(
        compute,
        mesh=fine,
        in_specs=(P(dp, None), both, both, both, both, both),
        out_specs=(both, P(dp, None), both, both),
        check_vma=False,
    )
```

```python
import jax
import jax.numpy as jnp
import numpy as np
from jax import lax
from jax.experimental import pallas as pl
from jax.experimental.pallas import tpu as pltpu
from jax.sharding import Mesh
from jax.sharding import PartitionSpec as P


BLOCK = 64
BF16 = jnp.bfloat16
F32 = jnp.float32
YH, X, CORE, Z, YL = 4, 4, 2, 8, 2
PIECES = 1
VM = pl.BlockSpec(memory_space=pltpu.VMEM)
HB = pl.BlockSpec(memory_space=pltpu.HBM)
SM = pl.BlockSpec(memory_space=pltpu.SMEM)


def keep_row(mask_ref, width):
    column = lax.broadcasted_iota(jnp.int32, (1, width), 1) // BLOCK
    keep = jnp.zeros((1, width), F32)
    for block in range(width // BLOCK):
        keep = jnp.where(column == block, mask_ref[0, block].astype(F32), keep)
    return keep


def mask_kernel(gm_hbm, um_hbm, gw_hbm, uw_hbm, out, gm, um, gw, uw, sems):
    moves = [
        pltpu.make_async_copy(source, target, sems.at[index])
        for index, (source, target) in enumerate(
            ((gw_hbm, gw), (uw_hbm, uw), (gm_hbm, gm), (um_hbm, um))
        )
    ]
    for move in moves:
        move.start()
    for move in moves:
        move.wait()
    width = gw.shape[1]
    gate = gw[...].astype(F32) * keep_row(gm, width)
    up = uw[...].astype(F32) * keep_row(um, width)
    both = jnp.concatenate([gate, up], axis=1).astype(BF16)
    for copy in range(YH):
        out[copy] = both


def prepare_kernel(tokens, ogt, tokens_out, grad_out):
    tokens_out[...] = tokens[...]
    grad_out[...] = ogt[...].astype(F32).T


def forward_kernel(place, tokens, grad_ref, *rest):
    mine, other = rest[:X], rest[X : 2 * X]
    hidden_t, d_both, *rest = rest[2 * X :]
    sends, keeps, w = rest[:PIECES], rest[PIECES:-1], rest[-1]
    core, half, own_x = place[0], place[1], place[2]
    width = grad_ref.shape[1]
    for yh in range(YH):
        for back in range(X):
            x = lax.rem(own_x + (X - back), X)
            w[yh * X + x, core] = mine[back][yh]
            w[yh * X + x, 1 - core] = other[back][yh]
    weights = w[...].reshape(YH * X * CORE * BLOCK, 2 * width)
    preact = jnp.dot(tokens[...], weights, preferred_element_type=F32)
    gate = preact[:, :width]
    up = preact[:, width:]
    sigmoid = jax.nn.sigmoid(gate)
    activation = gate * sigmoid
    hidden_t[...] = (activation * up).T
    grad = grad_ref[...]
    d_gate = grad * up * sigmoid * (1.0 + gate * (1.0 - sigmoid))
    d_up = grad * activation
    d_both[...] = jnp.concatenate([d_gate, d_up], axis=1).astype(BF16)
    rows, columns = sends[0].shape
    for index, outs in ((1 - half, sends), (half, keeps)):
        part = d_both[pl.ds(pl.multiple_of(index * rows, rows), rows), :]
        for piece, out in enumerate(outs):
            out[...] = lax.dot_general(
                part,
                weights[piece * columns : (piece + 1) * columns],
                (((1,), (1,)), ((), ())),
                preferred_element_type=F32,
            ).astype(BF16)


def weight_kernel(place, tokens, d_both, keep, send):
    core, own_x, own_yh = place[0], place[2], place[3]
    rows = CORE * BLOCK * 2
    for step in range(YH * X // 2):
        both = lax.dot_general(
            tokens[:, step * rows : (step + 1) * rows],
            d_both[...],
            (((0,), (0,)), ((), ())),
            preferred_element_type=F32,
        ).astype(BF16)
        for pair in range(2):
            yh, x = divmod(step * 2 + pair, X)
            ahead = lax.rem(x + X - own_x, X), lax.rem(yh + YH - own_yh, YH)
            low = both[pair * 128 : pair * 128 + 64]
            high = both[pair * 128 + 64 : pair * 128 + 128]
            first = core == 0
            keep[ahead] = jnp.where(first, low, high)
            send[ahead] = jnp.where(first, high, low)


def final_kernel(gm, um, *refs):
    parts, (grad_gate, grad_up) = refs[:-2], refs[-2:]
    width = grad_gate.shape[1]
    total = parts[0][...].astype(F32)
    for part in parts[1:]:
        total = total + part[...].astype(F32)
    grad_gate[...] = total[:, :width] * keep_row(gm, width)
    grad_up[...] = total[:, width:] * keep_row(um, width)


def pair_kernel(first, second, *outs):
    for index, out in enumerate(outs):
        out[...] = (first[index].astype(F32) + second[index].astype(F32)).astype(BF16)


def rows_kernel(*refs):
    parts, outs = refs[:X], refs[X:]
    for index, out in enumerate(outs):
        total = parts[0][index].astype(F32)
        for part in parts[1:]:
            total = total + part[index].astype(F32)
        out[...] = total.astype(BF16)


def add_kernel(first, second, out):
    out[...] = (first[...].astype(F32) + second[...].astype(F32)).astype(BF16)


def total_of(parts):
    total = parts[0].astype(F32)
    for source in range(1, parts.shape[0]):
        total = total + parts[source].astype(F32)
    return total.astype(BF16)


def sum_copies_kernel(parts, out):
    total = total_of(parts)
    for copy in range(out.shape[0]):
        out[copy] = total


def join_kernel(place, *refs):
    mine, other, out = refs[:PIECES], refs[PIECES:-1], refs[-1]
    half = place[1]
    rows, columns = mine[0].shape
    for piece in range(PIECES):
        span = slice(piece * columns, (piece + 1) * columns)
        out[pl.ds(pl.multiple_of(half * rows, rows), rows), span] = mine[piece][...]
        out[pl.ds(pl.multiple_of((1 - half) * rows, rows), rows), span] = other[piece][...]


def shape(dims, dtype=BF16):
    return jax.ShapeDtypeStruct(dims, dtype)


def params():
    return pltpu.CompilerParams(vmem_limit_bytes=40 << 20)


def swap(array, axis):
    return lax.ppermute(array, axis, [(0, 1), (1, 0)])


def shift(array, axis, size, steps):
    return lax.ppermute(array, axis, [(i, (i + steps) % size) for i in range(size)])


def call(kernel, out_shape, *operands, scalars=0, scratch=()):
    many = isinstance(out_shape, list)
    results = pl.pallas_call(
        kernel,
        in_specs=[SM] * scalars + [VM] * (len(operands) - scalars),
        out_specs=[VM] * len(out_shape) if many else VM,
        out_shape=out_shape,
        scratch_shapes=list(scratch),
        compiler_params=params(),
    )(*operands)
    return list(results) if many else results


def compute(tokens, out_grad, gate_weight, up_weight, gate_mask, up_mask):
    width = gate_weight.shape[1]
    count, features = tokens.shape
    half = count // YL
    chunk = half // Z
    columns = features // PIECES
    place = jnp.stack([lax.axis_index(name) for name in ("core", "yl", "x", "yh")])
    copies = pl.pallas_call(
        mask_kernel,
        in_specs=[HB] * 4,
        out_specs=VM,
        out_shape=shape((YH, BLOCK, 2 * width)),
        scratch_shapes=[
            pltpu.SMEM(gate_mask.shape, jnp.int32),
            pltpu.SMEM(up_mask.shape, jnp.int32),
            pltpu.VMEM(gate_weight.shape, BF16),
            pltpu.VMEM(up_weight.shape, BF16),
            pltpu.SemaphoreType.DMA((4,)),
        ],
    )(gate_mask, up_mask, gate_weight, up_weight)
    rows = lax.all_to_all(copies, "yh", 0, 0, tiled=True)
    mine, other = [rows], []
    for steps in range(1, X):
        mine.append(shift(rows, "x", X, steps))
    for steps in range(X):
        other.append(swap(mine[steps], "core"))
    tokens, grad = call(
        prepare_kernel, [shape(tokens.shape), shape((count, width), F32)], tokens, out_grad.T
    )
    hidden_t, d_both, *partials = call(
        forward_kernel,
        [shape((width, count), F32), shape((count, 2 * width))]
        + [shape((half, columns))] * (2 * PIECES),
        place,
        tokens,
        grad,
        *mine,
        *other,
        scalars=1,
        scratch=[pltpu.VMEM((YH * X, CORE, BLOCK, 2 * width), BF16)],
    )
    sends, keeps = partials[:PIECES], partials[PIECES:]
    received = []
    for piece in range(PIECES):
        received.append(swap(sends[piece], "yl"))
    w_keep, w_send = call(
        weight_kernel,
        [shape((X, YH, BLOCK, 2 * width))] * 2,
        place,
        tokens,
        d_both,
        scalars=1,
    )
    w_received = swap(w_send, "core")
    w_parts = call(
        pair_kernel, [shape((YH, BLOCK, 2 * width))] * X, w_keep, w_received
    )
    for steps in range(1, X):
        w_parts[steps] = shift(w_parts[steps], "x", X, steps)
    w_parts = call(rows_kernel, [shape((BLOCK, 2 * width))] * YH, *w_parts)
    for steps in range(1, YH):
        w_parts[steps] = shift(w_parts[steps], "yh", YH, steps)
    grad_gate, grad_up = call(
        final_kernel,
        [shape((BLOCK, width), F32)] * 2,
        gate_mask,
        up_mask,
        *w_parts,
        scalars=2,
    )
    own, others = [], []
    for piece in range(PIECES):
        x_sum = call(add_kernel, shape((half, columns)), keeps[piece], received[piece])
        x_parts = lax.all_to_all(x_sum.reshape(Z, chunk, columns), "z", 0, 0, tiled=True)
        x_copies = call(sum_copies_kernel, shape((Z, chunk, columns)), x_parts)
        x_half = lax.all_to_all(x_copies, "z", 0, 0, tiled=True).reshape(half, columns)
        own.append(x_half)
        others.append(swap(x_half, "yl"))
    grad_tokens = call(
        join_kernel, shape((count, features)), place, *own, *others, scalars=1
    )
    return (hidden_t.T, grad_tokens, grad_gate, grad_up)


def solution(mesh):
    fine = Mesh(
        np.asarray(mesh.devices).reshape(YH, X, CORE, Z, YL), ("yh", "x", "core", "z", "yl")
    )
    dp = ("yh", "x", "core")
    tensor = ("z", "yl")
    both = P(dp, tensor)
    return jax.shard_map(
        compute,
        mesh=fine,
        in_specs=(P(dp, None), both, both, both, both, both),
        out_specs=(both, P(dp, None), both, both),
        check_vma=False,
    )
```

```python
import jax
import jax.numpy as jnp
import numpy as np
from jax import lax
from jax.experimental import pallas as pl
from jax.experimental.pallas import tpu as pltpu
from jax.sharding import Mesh
from jax.sharding import PartitionSpec as P


BLOCK = 64
BF16 = jnp.bfloat16
F32 = jnp.float32
YH, X, CORE, Z, YL = 4, 4, 2, 8, 2
FIRST = 1536
VM = pl.BlockSpec(memory_space=pltpu.VMEM)
HB = pl.BlockSpec(memory_space=pltpu.HBM)
SM = pl.BlockSpec(memory_space=pltpu.SMEM)


def keep_row(mask_ref, width):
    column = lax.broadcasted_iota(jnp.int32, (1, width), 1) // BLOCK
    keep = jnp.zeros((1, width), F32)
    for block in range(width // BLOCK):
        keep = jnp.where(column == block, mask_ref[0, block].astype(F32), keep)
    return keep


def mask_kernel(gm_hbm, um_hbm, gw_hbm, uw_hbm, out, gm, um, gw, uw, sems):
    moves = [
        pltpu.make_async_copy(source, target, sems.at[index])
        for index, (source, target) in enumerate(
            ((gw_hbm, gw), (uw_hbm, uw), (gm_hbm, gm), (um_hbm, um))
        )
    ]
    for move in moves:
        move.start()
    for move in moves:
        move.wait()
    width = gw.shape[1]
    gate = gw[...].astype(F32) * keep_row(gm, width)
    up = uw[...].astype(F32) * keep_row(um, width)
    both = jnp.concatenate([gate, up], axis=1).astype(BF16)
    for copy in range(YH):
        out[copy] = both


def prepare_kernel(tokens, ogt, tokens_out, grad_out):
    tokens_out[...] = tokens[...]
    grad_out[...] = ogt[...].astype(F32).T


def forward_kernel(place, tokens, grad_ref, *rest):
    mine, other = rest[:X], rest[X : 2 * X]
    hidden_t, d_both, send, keep, side, w = rest[2 * X :]
    core, half, own_x = place[0], place[1], place[2]
    width = grad_ref.shape[1]
    for yh in range(YH):
        for back in range(X):
            x = lax.rem(own_x + (X - back), X)
            row = (yh * X + x) * CORE * BLOCK
            for rows, index in ((mine[back], core), (other[back], 1 - core)):
                start = pl.multiple_of(row + index * BLOCK, BLOCK)
                w[pl.ds(start, BLOCK), :] = rows[yh]
    weights = w[...]
    preact = jnp.dot(tokens[...], weights, preferred_element_type=F32)
    gate = preact[:, :width]
    up = preact[:, width:]
    sigmoid = jax.nn.sigmoid(gate)
    activation = gate * sigmoid
    hidden_t[...] = (activation * up).T
    grad = grad_ref[...]
    d_gate = grad * up * sigmoid * (1.0 + gate * (1.0 - sigmoid))
    d_up = grad * activation
    d_both[...] = jnp.concatenate([d_gate, d_up], axis=1).astype(BF16)
    rows = send.shape[0]
    for out, index in ((send, 1 - half), (keep, half)):
        start = pl.multiple_of(index * rows, rows)
        out[...] = to_tokens(d_both[pl.ds(start, rows), :], weights[:FIRST])
    side[...] = to_tokens(d_both[...], weights[FIRST:])


def to_tokens(grad, weights):
    return lax.dot_general(
        grad, weights, (((1,), (1,)), ((), ())), preferred_element_type=F32
    ).astype(BF16)


def weight_kernel(place, tokens, d_both, keep, send):
    core, own_x, own_yh = place[0], place[2], place[3]
    rows = CORE * BLOCK * 2
    for step in range(YH * X // 2):
        both = lax.dot_general(
            tokens[:, step * rows : (step + 1) * rows],
            d_both[...],
            (((0,), (0,)), ((), ())),
            preferred_element_type=F32,
        ).astype(BF16)
        for pair in range(2):
            yh, x = divmod(step * 2 + pair, X)
            ahead = lax.rem(x + X - own_x, X), lax.rem(yh + YH - own_yh, YH)
            low = both[pair * 128 : pair * 128 + 64]
            high = both[pair * 128 + 64 : pair * 128 + 128]
            first = core == 0
            keep[ahead] = jnp.where(first, low, high)
            send[ahead] = jnp.where(first, high, low)


def final_kernel(gm, um, *refs):
    parts, (grad_gate, grad_up) = refs[:-2], refs[-2:]
    width = grad_gate.shape[1]
    total = parts[0][...].astype(F32)
    for part in parts[1:]:
        total = total + part[...].astype(F32)
    grad_gate[...] = total[:, :width] * keep_row(gm, width)
    grad_up[...] = total[:, width:] * keep_row(um, width)


def pair_kernel(first, second, *outs):
    for index, out in enumerate(outs):
        out[...] = (first[index].astype(F32) + second[index].astype(F32)).astype(BF16)


def rows_kernel(*refs):
    parts, outs = refs[:X], refs[X:]
    for index, out in enumerate(outs):
        total = parts[0][index].astype(F32)
        for part in parts[1:]:
            total = total + part[index].astype(F32)
        out[...] = total.astype(BF16)


def add_kernel(first, second, out):
    out[...] = (first[...].astype(F32) + second[...].astype(F32)).astype(BF16)


def total_of(parts):
    total = parts[0].astype(F32)
    for source in range(1, parts.shape[0]):
        total = total + parts[source].astype(F32)
    return total.astype(BF16)


def sum_kernel(parts, out):
    out[...] = total_of(parts)


def sum_copies_kernel(parts, out):
    total = total_of(parts)
    for copy in range(out.shape[0]):
        out[copy] = total


def add_copies_kernel(first, second, out):
    total = (first[...].astype(F32) + second[...].astype(F32)).astype(BF16)
    for copy in range(out.shape[0]):
        out[copy] = total


def join_kernel(place, mine, other, side, out):
    half = place[1]
    rows = mine.shape[0]
    out[pl.ds(pl.multiple_of(half * rows, rows), rows), :FIRST] = mine[...]
    out[pl.ds(pl.multiple_of((1 - half) * rows, rows), rows), :FIRST] = other[...]
    out[:, FIRST:] = side[...]


def shape(dims, dtype=BF16):
    return jax.ShapeDtypeStruct(dims, dtype)


def params():
    return pltpu.CompilerParams(vmem_limit_bytes=40 << 20)


def swap(array, axis):
    return lax.ppermute(array, axis, [(0, 1), (1, 0)])


def shift(array, axis, size, steps):
    return lax.ppermute(array, axis, [(i, (i + steps) % size) for i in range(size)])


def call(kernel, out_shape, *operands, scalars=0, scratch=()):
    many = isinstance(out_shape, list)
    results = pl.pallas_call(
        kernel,
        in_specs=[SM] * scalars + [VM] * (len(operands) - scalars),
        out_specs=[VM] * len(out_shape) if many else VM,
        out_shape=out_shape,
        scratch_shapes=list(scratch),
        compiler_params=params(),
    )(*operands)
    return list(results) if many else results


def compute(tokens, out_grad, gate_weight, up_weight, gate_mask, up_mask):
    width = gate_weight.shape[1]
    count, features = tokens.shape
    half = count // YL
    chunk = half // Z
    rest = features - FIRST
    place = jnp.stack([lax.axis_index(name) for name in ("core", "yl", "x", "yh")])
    copies = pl.pallas_call(
        mask_kernel,
        in_specs=[HB] * 4,
        out_specs=VM,
        out_shape=shape((YH, BLOCK, 2 * width)),
        scratch_shapes=[
            pltpu.SMEM(gate_mask.shape, jnp.int32),
            pltpu.SMEM(up_mask.shape, jnp.int32),
            pltpu.VMEM(gate_weight.shape, BF16),
            pltpu.VMEM(up_weight.shape, BF16),
            pltpu.SemaphoreType.DMA((4,)),
        ],
    )(gate_mask, up_mask, gate_weight, up_weight)
    rows = lax.all_to_all(copies, "yh", 0, 0, tiled=True)
    mine, other = [rows], []
    for steps in range(1, X):
        mine.append(shift(rows, "x", X, steps))
    for steps in range(X):
        other.append(swap(mine[steps], "core"))
    tokens, grad = call(
        prepare_kernel, [shape(tokens.shape), shape((count, width), F32)], tokens, out_grad.T
    )
    hidden_t, d_both, send, keep, side = call(
        forward_kernel,
        [
            shape((width, count), F32),
            shape((count, 2 * width)),
            shape((half, FIRST)),
            shape((half, FIRST)),
            shape((count, rest)),
        ],
        place,
        tokens,
        grad,
        *mine,
        *other,
        scalars=1,
        scratch=[pltpu.VMEM((features, 2 * width), BF16)],
    )
    received = swap(send, "yl")
    side = lax.all_to_all(side.reshape(Z, 2 * chunk, rest), "z", 0, 0, tiled=True)
    w_keep, w_send = call(
        weight_kernel,
        [shape((X, YH, BLOCK, 2 * width))] * 2,
        place,
        tokens,
        d_both,
        scalars=1,
    )
    w_received = swap(w_send, "core")
    w_parts = call(pair_kernel, [shape((YH, BLOCK, 2 * width))] * X, w_keep, w_received)
    for steps in range(1, X):
        w_parts[steps] = shift(w_parts[steps], "x", X, steps)
    w_parts = call(rows_kernel, [shape((BLOCK, 2 * width))] * YH, *w_parts)
    for steps in range(1, YH):
        w_parts[steps] = shift(w_parts[steps], "yh", YH, steps)
    grad_gate, grad_up = call(
        final_kernel,
        [shape((BLOCK, width), F32)] * 2,
        gate_mask,
        up_mask,
        *w_parts,
        scalars=2,
    )
    main = call(add_kernel, shape((half, FIRST)), keep, received)
    main = lax.all_to_all(main.reshape(Z, chunk, FIRST), "z", 0, 0, tiled=True)
    side = call(sum_kernel, shape((2 * chunk, rest)), side)
    side_other = swap(side, "yl")
    side = call(add_copies_kernel, shape((Z, 2 * chunk, rest)), side, side_other)
    main = call(sum_copies_kernel, shape((Z, chunk, FIRST)), main)
    main = lax.all_to_all(main, "z", 0, 0, tiled=True).reshape(half, FIRST)
    main_other = swap(main, "yl")
    side = lax.all_to_all(side, "z", 0, 0, tiled=True).reshape(count, rest)
    grad_tokens = call(
        join_kernel, shape((count, features)), place, main, main_other, side, scalars=1
    )
    return (hidden_t.T, grad_tokens, grad_gate, grad_up)


def solution(mesh):
    fine = Mesh(
        np.asarray(mesh.devices).reshape(YH, X, CORE, Z, YL), ("yh", "x", "core", "z", "yl")
    )
    dp = ("yh", "x", "core")
    tensor = ("z", "yl")
    both = P(dp, tensor)
    return jax.shard_map(
        compute,
        mesh=fine,
        in_specs=(P(dp, None), both, both, both, both, both),
        out_specs=(both, P(dp, None), both, both),
        check_vma=False,
    )
```

```python
import jax
import jax.numpy as jnp
import numpy as np
from jax import lax
from jax.experimental import pallas as pl
from jax.experimental.pallas import tpu as pltpu
from jax.sharding import Mesh
from jax.sharding import PartitionSpec as P


BLOCK = 64
BF16 = jnp.bfloat16
F32 = jnp.float32
YH, X, CORE, Z, YL = 4, 4, 2, 8, 2
FIRST = 1536
VM = pl.BlockSpec(memory_space=pltpu.VMEM)
HB = pl.BlockSpec(memory_space=pltpu.HBM)
SM = pl.BlockSpec(memory_space=pltpu.SMEM)


def keep_row(mask_ref, width):
    column = lax.broadcasted_iota(jnp.int32, (1, width), 1) // BLOCK
    keep = jnp.zeros((1, width), F32)
    for block in range(width // BLOCK):
        keep = jnp.where(column == block, mask_ref[0, block].astype(F32), keep)
    return keep


def mask_kernel(gm_hbm, um_hbm, gw_hbm, uw_hbm, out, gm, um, gw, uw, sems):
    moves = [
        pltpu.make_async_copy(source, target, sems.at[index])
        for index, (source, target) in enumerate(
            ((gw_hbm, gw), (uw_hbm, uw), (gm_hbm, gm), (um_hbm, um))
        )
    ]
    for move in moves:
        move.start()
    for move in moves:
        move.wait()
    width = gw.shape[1]
    gate = gw[...].astype(F32) * keep_row(gm, width)
    up = uw[...].astype(F32) * keep_row(um, width)
    both = jnp.concatenate([gate, up], axis=1).astype(BF16)
    for copy in range(YH):
        out[copy] = both


def prepare_kernel(tokens, ogt, tokens_out, grad_out):
    tokens_out[...] = tokens[...]
    grad_out[...] = ogt[...].astype(F32).T


def forward_kernel(place, tokens, grad_ref, *rest):
    mine, other = rest[:X], rest[X : 2 * X]
    hidden_t, d_both, send, w = rest[2 * X :]
    core, half, own_x = place[0], place[1], place[2]
    width = grad_ref.shape[1]
    for yh in range(YH):
        for back in range(X):
            x = lax.rem(own_x + (X - back), X)
            row = (yh * X + x) * CORE * BLOCK
            for rows, index in ((mine[back], core), (other[back], 1 - core)):
                start = pl.multiple_of(row + index * BLOCK, BLOCK)
                w[pl.ds(start, BLOCK), :] = rows[yh]
    weights = w[...]
    preact = jnp.dot(tokens[...], weights, preferred_element_type=F32)
    gate = preact[:, :width]
    up = preact[:, width:]
    sigmoid = jax.nn.sigmoid(gate)
    activation = gate * sigmoid
    hidden_t[...] = (activation * up).T
    grad = grad_ref[...]
    d_gate = grad * up * sigmoid * (1.0 + gate * (1.0 - sigmoid))
    d_up = grad * activation
    d_both[...] = jnp.concatenate([d_gate, d_up], axis=1).astype(BF16)
    rows = send.shape[0]
    start = pl.multiple_of((1 - half) * rows, rows)
    send[...] = to_tokens(d_both[pl.ds(start, rows), :], weights[:FIRST])


def to_tokens(grad, weights):
    return lax.dot_general(
        grad, weights, (((1,), (1,)), ((), ())), preferred_element_type=F32
    ).astype(BF16)


def weight_kernel(place, tokens, d_both, weights, keep, send, main, side):
    part = main.shape[0]
    start = pl.multiple_of(place[1] * part, part)
    side[...] = to_tokens(d_both[...], weights[FIRST:, :])
    main[...] = to_tokens(d_both[pl.ds(start, part), :], weights[:FIRST, :])
    core, own_x = place[0], place[2]
    rows = CORE * BLOCK * 2
    for step in range(YH * X // 2):
        both = lax.dot_general(
            tokens[:, step * rows : (step + 1) * rows],
            d_both[...],
            (((0,), (0,)), ((), ())),
            preferred_element_type=F32,
        ).astype(BF16)
        for pair in range(2):
            yh, x = divmod(step * 2 + pair, X)
            ahead = lax.rem(x + X - own_x, X), yh
            low = both[pair * 128 : pair * 128 + 64]
            high = both[pair * 128 + 64 : pair * 128 + 128]
            first = core == 0
            keep[ahead] = jnp.where(first, low, high)
            send[ahead] = jnp.where(first, high, low)


def final_kernel(gm, um, parts, grad_gate, grad_up):
    width = grad_gate.shape[1]
    total = parts[0].astype(F32)
    for source in range(1, YH):
        total = total + parts[source].astype(F32)
    grad_gate[...] = total[:, :width] * keep_row(gm, width)
    grad_up[...] = total[:, width:] * keep_row(um, width)


def pair_kernel(first, second, *outs):
    for index, out in enumerate(outs):
        out[...] = (first[index].astype(F32) + second[index].astype(F32)).astype(BF16)


def x_sum_kernel(*refs):
    parts, out = refs[:-1], refs[-1]
    total = parts[0][...].astype(F32)
    for part in parts[1:]:
        total = total + part[...].astype(F32)
    out[...] = total.astype(BF16)


def add_kernel(first, second, out):
    out[...] = (first[...].astype(F32) + second[...].astype(F32)).astype(BF16)


def total_of(parts):
    total = parts[0].astype(F32)
    for source in range(1, parts.shape[0]):
        total = total + parts[source].astype(F32)
    return total.astype(BF16)


def side_kernel(place, parts, keep, send):
    half = place[1]
    rows = keep.shape[0]
    total = total_of(parts)
    low, high = total[:rows], total[rows:]
    keep[...] = jnp.where(half == 0, low, high)
    send[...] = jnp.where(half == 0, high, low)


def main_kernel(parts, side, side_other, out):
    total = total_of(parts)
    rest = (side[...].astype(F32) + side_other[...].astype(F32)).astype(BF16)
    for copy in range(out.shape[0]):
        out[copy, :, :FIRST] = total
        out[copy, :, FIRST:] = rest


def join_kernel(place, mine, other, out):
    half = place[1]
    chunk = mine.shape[1]
    for part, index in ((mine, half), (other, 1 - half)):
        for z in range(Z):
            start = pl.multiple_of((index * Z + z) * chunk, chunk)
            out[pl.ds(start, chunk), :FIRST] = part[z, :, :FIRST]
            start = pl.multiple_of((z * YL + index) * chunk, chunk)
            out[pl.ds(start, chunk), FIRST:] = part[z, :, FIRST:]


def shape(dims, dtype=BF16):
    return jax.ShapeDtypeStruct(dims, dtype)


def params():
    return pltpu.CompilerParams(vmem_limit_bytes=40 << 20)


def swap(array, axis):
    return lax.ppermute(array, axis, [(0, 1), (1, 0)])


def shift(array, axis, size, steps):
    return lax.ppermute(array, axis, [(i, (i + steps) % size) for i in range(size)])


def call(kernel, out_shape, *operands, scalars=0, scratch=()):
    many = isinstance(out_shape, list)
    results = pl.pallas_call(
        kernel,
        in_specs=[SM] * scalars + [VM] * (len(operands) - scalars),
        out_specs=[VM] * len(out_shape) if many else VM,
        out_shape=out_shape,
        scratch_shapes=list(scratch),
        compiler_params=params(),
    )(*operands)
    return list(results) if many else results


def compute(tokens, out_grad, gate_weight, up_weight, gate_mask, up_mask):
    width = gate_weight.shape[1]
    count, features = tokens.shape
    half = count // YL
    chunk = half // Z
    rest = features - FIRST
    place = jnp.stack([lax.axis_index(name) for name in ("core", "yl", "x")])
    copies = pl.pallas_call(
        mask_kernel,
        in_specs=[HB] * 4,
        out_specs=VM,
        out_shape=shape((YH, BLOCK, 2 * width)),
        scratch_shapes=[
            pltpu.SMEM(gate_mask.shape, jnp.int32),
            pltpu.SMEM(up_mask.shape, jnp.int32),
            pltpu.VMEM(gate_weight.shape, BF16),
            pltpu.VMEM(up_weight.shape, BF16),
            pltpu.SemaphoreType.DMA((4,)),
        ],
    )(gate_mask, up_mask, gate_weight, up_weight)
    rows = lax.all_to_all(copies, "yh", 0, 0, tiled=True)
    mine, other = [rows], []
    for steps in range(1, X):
        mine.append(shift(rows, "x", X, steps))
    for steps in range(X):
        other.append(swap(mine[steps], "core"))
    tokens, grad = call(
        prepare_kernel, [shape(tokens.shape), shape((count, width), F32)], tokens, out_grad.T
    )
    hidden_t, d_both, send, weights = call(
        forward_kernel,
        [
            shape((width, count), F32),
            shape((count, 2 * width)),
            shape((half, FIRST)),
            shape((features, 2 * width)),
        ],
        place,
        tokens,
        grad,
        *mine,
        *other,
        scalars=1,
    )
    received = swap(send, "yl")
    w_keep, w_send, keep, side = call(
        weight_kernel,
        [shape((X, YH, BLOCK, 2 * width))] * 2 + [shape((half, FIRST)), shape((count, rest))],
        place,
        tokens,
        d_both,
        weights,
        scalars=1,
    )
    side = lax.all_to_all(side.reshape(Z, 2 * chunk, rest), "z", 0, 0, tiled=True)
    w_received = swap(w_send, "core")
    w_parts = call(pair_kernel, [shape((YH, BLOCK, 2 * width))] * X, w_keep, w_received)
    for steps in range(1, X):
        w_parts[steps] = shift(w_parts[steps], "x", X, steps)
    w_sum = call(x_sum_kernel, shape((YH, BLOCK, 2 * width)), *w_parts)
    w_parts = lax.all_to_all(w_sum, "yh", 0, 0, tiled=True)
    grad_gate, grad_up = call(
        final_kernel,
        [shape((BLOCK, width), F32)] * 2,
        gate_mask,
        up_mask,
        w_parts,
        scalars=2,
    )
    main = call(add_kernel, shape((half, FIRST)), keep, received)
    main = lax.all_to_all(main.reshape(Z, chunk, FIRST), "z", 0, 0, tiled=True)
    side, side_send = call(
        side_kernel, [shape((chunk, rest))] * 2, place, side, scalars=1
    )
    side_other = swap(side_send, "yl")
    main = call(main_kernel, shape((Z, chunk, features)), main, side, side_other)
    main = lax.all_to_all(main, "z", 0, 0, tiled=True)
    main_other = swap(main, "yl")
    grad_tokens = call(
        join_kernel, shape((count, features)), place, main, main_other, scalars=1
    )
    return (hidden_t.T, grad_tokens, grad_gate, grad_up)


def solution(mesh):
    fine = Mesh(
        np.asarray(mesh.devices).reshape(YH, X, CORE, Z, YL), ("yh", "x", "core", "z", "yl")
    )
    dp = ("yh", "x", "core")
    tensor = ("z", "yl")
    both = P(dp, tensor)
    return jax.shard_map(
        compute,
        mesh=fine,
        in_specs=(P(dp, None), both, both, both, both, both),
        out_specs=(both, P(dp, None), both, both),
        check_vma=False,
    )
```

```python
import jax
import jax.numpy as jnp
import numpy as np
from jax import lax
from jax.experimental import pallas as pl
from jax.experimental.pallas import tpu as pltpu
from jax.sharding import Mesh
from jax.sharding import PartitionSpec as P


BLOCK = 64
BF16 = jnp.bfloat16
F32 = jnp.float32
YH, X, CORE, Z, YL = 4, 4, 2, 8, 2
FIRST = 1536
VM = pl.BlockSpec(memory_space=pltpu.VMEM)
HB = pl.BlockSpec(memory_space=pltpu.HBM)
ANY = pl.BlockSpec(memory_space=pl.ANY)
SM = pl.BlockSpec(memory_space=pltpu.SMEM)


def keep_row(mask_ref, width):
    column = lax.broadcasted_iota(jnp.int32, (1, width), 1) // BLOCK
    keep = jnp.zeros((1, width), F32)
    for block in range(width // BLOCK):
        keep = jnp.where(column == block, mask_ref[0, block].astype(F32), keep)
    return keep


def mask_kernel(gm_hbm, um_hbm, gw_hbm, uw_hbm, out, gm, um, gw, uw, sems):
    moves = [
        pltpu.make_async_copy(source, target, sems.at[index])
        for index, (source, target) in enumerate(
            ((gw_hbm, gw), (uw_hbm, uw), (gm_hbm, gm), (um_hbm, um))
        )
    ]
    for move in moves:
        move.start()
    for move in moves:
        move.wait()
    width = gw.shape[1]
    gate = gw[...].astype(F32) * keep_row(gm, width)
    up = uw[...].astype(F32) * keep_row(um, width)
    both = jnp.concatenate([gate, up], axis=1).astype(BF16)
    for copy in range(YH):
        out[copy] = both


def prepare_kernel(tokens, ogt, tokens_out, grad_out):
    tokens_out[...] = tokens[...]
    grad_out[...] = ogt[...].astype(F32).T


def forward_kernel(place, tokens, grad_ref, *rest):
    pieces = (rest[:X], rest[X : 2 * X])
    hidden_out, send_out, keep_out, side_out, d_both, *scratch = rest[2 * X :]
    w, preact_ref, hidden_t, send, keep, side, sems, out_sems = scratch
    outs = []

    def put(source, target):
        outs.append(pltpu.make_async_copy(source, target, out_sems.at[len(outs)]))
        outs[-1].start()

    core, half, own_x = place[0], place[1], place[2]
    width = grad_ref.shape[1]
    group = X * CORE * BLOCK
    moves = []
    for yh in range(YH):
        for back in range(X):
            x = lax.rem(own_x + (X - back), X)
            row = yh * group + x * CORE * BLOCK
            for index, place_of in enumerate((core, 1 - core)):
                start = pl.multiple_of(row + place_of * BLOCK, BLOCK)
                moves.append(
                    pltpu.make_async_copy(
                        pieces[index][back].at[yh],
                        w.at[pl.ds(start, BLOCK), :],
                        sems.at[len(moves)],
                    )
                )
    for move in moves:
        move.start()
    for yh in range(YH):
        for move in moves[yh * CORE * X : (yh + 1) * CORE * X]:
            move.wait()
        span = slice(yh * group, (yh + 1) * group)
        part = jnp.dot(tokens[:, span], w[span, :], preferred_element_type=F32)
        preact_ref[...] = part if yh == 0 else preact_ref[...] + part
    preact = preact_ref[...]
    weights = w[...]
    gate = preact[:, :width]
    up = preact[:, width:]
    sigmoid = jax.nn.sigmoid(gate)
    activation = gate * sigmoid
    hidden_t[...] = (activation * up).T
    put(hidden_t, hidden_out)
    grad = grad_ref[...]
    d_gate = grad * up * sigmoid * (1.0 + gate * (1.0 - sigmoid))
    d_up = grad * activation
    d_both[...] = jnp.concatenate([d_gate, d_up], axis=1).astype(BF16)
    rows = send.shape[0]
    side[...] = to_tokens(d_both[...], weights[FIRST:])
    put(side, side_out)
    for part, target, index in ((keep, keep_out, half), (send, send_out, 1 - half)):
        start = pl.multiple_of(index * rows, rows)
        part[...] = to_tokens(d_both[pl.ds(start, rows), :], weights[:FIRST])
        put(part, target)
    for move in outs:
        move.wait()


def to_tokens(grad, weights):
    return lax.dot_general(
        grad, weights, (((1,), (1,)), ((), ())), preferred_element_type=F32
    ).astype(BF16)


def weight_kernel(place, tokens, d_both, keep, send):
    core, own_x, own_yh = place[0], place[2], place[3]
    rows = CORE * BLOCK * 2
    for step in range(YH * X // 2):
        both = lax.dot_general(
            tokens[:, step * rows : (step + 1) * rows],
            d_both[...],
            (((0,), (0,)), ((), ())),
            preferred_element_type=F32,
        ).astype(BF16)
        for pair in range(2):
            yh, x = divmod(step * 2 + pair, X)
            ahead = lax.rem(x + X - own_x, X), lax.rem(yh + YH - own_yh, YH)
            low = both[pair * 128 : pair * 128 + 64]
            high = both[pair * 128 + 64 : pair * 128 + 128]
            first = core == 0
            keep[ahead] = jnp.where(first, low, high)
            send[ahead] = jnp.where(first, high, low)


def final_kernel(gm, um, *refs):
    parts, (grad_gate, grad_up) = refs[:-2], refs[-2:]
    width = grad_gate.shape[1]
    total = parts[0][...].astype(F32)
    for part in parts[1:]:
        total = total + part[...].astype(F32)
    grad_gate[...] = total[:, :width] * keep_row(gm, width)
    grad_up[...] = total[:, width:] * keep_row(um, width)


def pair_kernel(first, second, *outs):
    for index, out in enumerate(outs):
        out[...] = (first[index].astype(F32) + second[index].astype(F32)).astype(BF16)


def rows_kernel(*refs):
    parts, outs = refs[:X], refs[X:]
    for index, out in enumerate(outs):
        total = parts[0][index].astype(F32)
        for part in parts[1:]:
            total = total + part[index].astype(F32)
        out[...] = total.astype(BF16)


def add_kernel(first, second, out):
    out[...] = (first[...].astype(F32) + second[...].astype(F32)).astype(BF16)


def total_of(parts):
    total = parts[0].astype(F32)
    for source in range(1, parts.shape[0]):
        total = total + parts[source].astype(F32)
    return total.astype(BF16)


def sum_kernel(parts, out):
    out[...] = total_of(parts)


def sum_copies_kernel(parts, out):
    total = total_of(parts)
    for copy in range(out.shape[0]):
        out[copy] = total


def add_copies_kernel(first, second, out):
    total = (first[...].astype(F32) + second[...].astype(F32)).astype(BF16)
    for copy in range(out.shape[0]):
        out[copy] = total


def join_kernel(place, mine, other, side, out):
    half = place[1]
    rows = mine.shape[0]
    out[pl.ds(pl.multiple_of(half * rows, rows), rows), :FIRST] = mine[...]
    out[pl.ds(pl.multiple_of((1 - half) * rows, rows), rows), :FIRST] = other[...]
    out[:, FIRST:] = side[...]


def shape(dims, dtype=BF16):
    return jax.ShapeDtypeStruct(dims, dtype)


def params():
    return pltpu.CompilerParams(vmem_limit_bytes=40 << 20)


def swap(array, axis):
    return lax.ppermute(array, axis, [(0, 1), (1, 0)])


def shift(array, axis, size, steps):
    return lax.ppermute(array, axis, [(i, (i + steps) % size) for i in range(size)])


def call(kernel, out_shape, *operands, scalars=0):
    many = isinstance(out_shape, list)
    results = pl.pallas_call(
        kernel,
        in_specs=[SM] * scalars + [VM] * (len(operands) - scalars),
        out_specs=[VM] * len(out_shape) if many else VM,
        out_shape=out_shape,
        compiler_params=params(),
    )(*operands)
    return list(results) if many else results


def compute(tokens, out_grad, gate_weight, up_weight, gate_mask, up_mask):
    width = gate_weight.shape[1]
    count, features = tokens.shape
    half = count // YL
    chunk = half // Z
    rest = features - FIRST
    place = jnp.stack([lax.axis_index(name) for name in ("core", "yl", "x", "yh")])
    copies = pl.pallas_call(
        mask_kernel,
        in_specs=[HB] * 4,
        out_specs=VM,
        out_shape=shape((YH, BLOCK, 2 * width)),
        scratch_shapes=[
            pltpu.SMEM(gate_mask.shape, jnp.int32),
            pltpu.SMEM(up_mask.shape, jnp.int32),
            pltpu.VMEM(gate_weight.shape, BF16),
            pltpu.VMEM(up_weight.shape, BF16),
            pltpu.SemaphoreType.DMA((4,)),
        ],
    )(gate_mask, up_mask, gate_weight, up_weight)
    rows = lax.all_to_all(copies, "yh", 0, 0, tiled=True)
    mine, other = [rows], []
    for steps in range(1, X):
        mine.append(shift(rows, "x", X, steps))
    for steps in range(X):
        other.append(swap(mine[steps], "core"))
    tokens, grad = call(
        prepare_kernel, [shape(tokens.shape), shape((count, width), F32)], tokens, out_grad.T
    )
    dims = [(width, count), (half, FIRST), (half, FIRST), (count, rest)]
    types = [F32, BF16, BF16, BF16]
    hidden_t, send, keep, side, d_both = pl.pallas_call(
        forward_kernel,
        in_specs=[SM, VM, VM] + [ANY] * (2 * X),
        out_specs=[HB] * 4 + [VM],
        out_shape=[shape(*pair) for pair in zip(dims, types)] + [shape((count, 2 * width))],
        scratch_shapes=[
            pltpu.VMEM((features, 2 * width), BF16),
            pltpu.VMEM((count, 2 * width), F32),
            *(pltpu.VMEM(*pair) for pair in zip(dims, types)),
            pltpu.SemaphoreType.DMA((YH * X * CORE,)),
            pltpu.SemaphoreType.DMA((4,)),
        ],
        compiler_params=params(),
    )(place, tokens, grad, *mine, *other)
    received = swap(send, "yl")
    side = lax.all_to_all(side.reshape(Z, 2 * chunk, rest), "z", 0, 0, tiled=True)
    w_keep, w_send = call(
        weight_kernel,
        [shape((X, YH, BLOCK, 2 * width))] * 2,
        place,
        tokens,
        d_both,
        scalars=1,
    )
    w_received = swap(w_send, "core")
    w_parts = call(pair_kernel, [shape((YH, BLOCK, 2 * width))] * X, w_keep, w_received)
    for steps in range(1, X):
        w_parts[steps] = shift(w_parts[steps], "x", X, steps)
    w_parts = call(rows_kernel, [shape((BLOCK, 2 * width))] * YH, *w_parts)
    for steps in range(1, YH):
        w_parts[steps] = shift(w_parts[steps], "yh", YH, steps)
    grad_gate, grad_up = call(
        final_kernel,
        [shape((BLOCK, width), F32)] * 2,
        gate_mask,
        up_mask,
        *w_parts,
        scalars=2,
    )
    main = call(add_kernel, shape((half, FIRST)), keep, received)
    main = lax.all_to_all(main.reshape(Z, chunk, FIRST), "z", 0, 0, tiled=True)
    side = call(sum_kernel, shape((2 * chunk, rest)), side)
    side_other = swap(side, "yl")
    side = call(add_copies_kernel, shape((Z, 2 * chunk, rest)), side, side_other)
    main = call(sum_copies_kernel, shape((Z, chunk, FIRST)), main)
    main = lax.all_to_all(main, "z", 0, 0, tiled=True).reshape(half, FIRST)
    main_other = swap(main, "yl")
    side = lax.all_to_all(side, "z", 0, 0, tiled=True).reshape(count, rest)
    grad_tokens = call(
        join_kernel, shape((count, features)), place, main, main_other, side, scalars=1
    )
    return (hidden_t.T, grad_tokens, grad_gate, grad_up)


def solution(mesh):
    fine = Mesh(
        np.asarray(mesh.devices).reshape(YH, X, CORE, Z, YL), ("yh", "x", "core", "z", "yl")
    )
    dp = ("yh", "x", "core")
    tensor = ("z", "yl")
    both = P(dp, tensor)
    return jax.shard_map(
        compute,
        mesh=fine,
        in_specs=(P(dp, None), both, both, both, both, both),
        out_specs=(both, P(dp, None), both, both),
        check_vma=False,
    )
```

```python
import jax
import jax.numpy as jnp
import numpy as np
from jax import lax
from jax.experimental import pallas as pl
from jax.experimental.pallas import tpu as pltpu
from jax.sharding import Mesh
from jax.sharding import PartitionSpec as P


BLOCK = 64
BF16 = jnp.bfloat16
F32 = jnp.float32
YH, X, CORE, Z, YL = 4, 4, 2, 8, 2
FIRST = 1536
VM = pl.BlockSpec(memory_space=pltpu.VMEM)
HB = pl.BlockSpec(memory_space=pltpu.HBM)
SM = pl.BlockSpec(memory_space=pltpu.SMEM)


def keep_row(mask_ref, width):
    column = lax.broadcasted_iota(jnp.int32, (1, width), 1) // BLOCK
    keep = jnp.zeros((1, width), F32)
    for block in range(width // BLOCK):
        keep = jnp.where(column == block, mask_ref[0, block].astype(F32), keep)
    return keep


def mask_kernel(gm_hbm, um_hbm, gw_hbm, uw_hbm, out, gm, um, gw, uw, sems):
    moves = [
        pltpu.make_async_copy(source, target, sems.at[index])
        for index, (source, target) in enumerate(
            ((gw_hbm, gw), (uw_hbm, uw), (gm_hbm, gm), (um_hbm, um))
        )
    ]
    for move in moves:
        move.start()
    for move in moves:
        move.wait()
    width = gw.shape[1]
    gate = gw[...].astype(F32) * keep_row(gm, width)
    up = uw[...].astype(F32) * keep_row(um, width)
    both = jnp.concatenate([gate, up], axis=1).astype(BF16)
    for copy in range(YH):
        out[copy] = both


def prepare_kernel(tokens, ogt, tokens_out, grad_out):
    tokens_out[...] = tokens[...]
    grad_out[...] = ogt[...].astype(F32).T.astype(BF16)


def forward_kernel(place, tokens, grad_ref, *rest):
    mine, other, hidden_t, d_both, send, keep, side, w = rest
    core, half = place[0], place[1]
    width = grad_ref.shape[1]
    for yh in range(YH):
        for x in range(X):
            row = (yh * X + x) * CORE * BLOCK
            for rows, index in ((mine, core), (other, 1 - core)):
                start = pl.multiple_of(row + index * BLOCK, BLOCK)
                w[pl.ds(start, BLOCK), :] = rows[x, yh]
    weights = w[...]
    preact = jnp.dot(tokens[...], weights, preferred_element_type=F32)
    gate = preact[:, :width]
    up = preact[:, width:]
    sigmoid = jax.nn.sigmoid(gate)
    activation = gate * sigmoid
    hidden_t[...] = (activation * up).T
    grad = grad_ref[...].astype(F32)
    d_gate = grad * up * sigmoid * (1.0 + gate * (1.0 - sigmoid))
    d_up = grad * activation
    d_both[...] = jnp.concatenate([d_gate, d_up], axis=1).astype(BF16)
    rows = send.shape[0]
    for out, index in ((send, 1 - half), (keep, half)):
        start = pl.multiple_of(index * rows, rows)
        out[...] = to_tokens(d_both[pl.ds(start, rows), :], weights[:FIRST])
    side[...] = to_tokens(d_both[...], weights[FIRST:])


def to_tokens(grad, weights):
    return lax.dot_general(
        grad, weights, (((1,), (1,)), ((), ())), preferred_element_type=F32
    ).astype(BF16)


def weight_kernel(place, tokens, d_both, keep, send):
    core, own_x, own_yh = place[0], place[2], place[3]
    rows = CORE * BLOCK * 2
    for step in range(YH * X // 2):
        both = lax.dot_general(
            tokens[:, step * rows : (step + 1) * rows],
            d_both[...],
            (((0,), (0,)), ((), ())),
            preferred_element_type=F32,
        ).astype(BF16)
        for pair in range(2):
            yh, x = divmod(step * 2 + pair, X)
            ahead = lax.rem(x + X - own_x, X), lax.rem(yh + YH - own_yh, YH)
            low = both[pair * 128 : pair * 128 + 64]
            high = both[pair * 128 + 64 : pair * 128 + 128]
            first = core == 0
            keep[ahead] = jnp.where(first, low, high)
            send[ahead] = jnp.where(first, high, low)


def final_kernel(gm, um, *refs):
    parts, (grad_gate, grad_up) = refs[:-2], refs[-2:]
    width = grad_gate.shape[1]
    total = parts[0][...].astype(F32)
    for part in parts[1:]:
        total = total + part[...].astype(F32)
    grad_gate[...] = total[:, :width] * keep_row(gm, width)
    grad_up[...] = total[:, width:] * keep_row(um, width)


def pair_kernel(first, second, *outs):
    for index, out in enumerate(outs):
        out[...] = (first[index].astype(F32) + second[index].astype(F32)).astype(BF16)


def rows_kernel(*refs):
    parts, outs = refs[:X], refs[X:]
    for index, out in enumerate(outs):
        total = parts[0][index].astype(F32)
        for part in parts[1:]:
            total = total + part[index].astype(F32)
        out[...] = total.astype(BF16)


def add_kernel(first, second, out):
    out[...] = (first[...].astype(F32) + second[...].astype(F32)).astype(BF16)


def total_of(parts):
    total = parts[0].astype(F32)
    for source in range(1, parts.shape[0]):
        total = total + parts[source].astype(F32)
    return total.astype(BF16)


def sum_kernel(parts, out):
    out[...] = total_of(parts)


def sum_copies_kernel(parts, out):
    total = total_of(parts)
    for copy in range(out.shape[0]):
        out[copy] = total


def add_copies_kernel(first, second, out):
    total = (first[...].astype(F32) + second[...].astype(F32)).astype(BF16)
    for copy in range(out.shape[0]):
        out[copy] = total


def join_kernel(place, mine, other, side, out):
    half = place[1]
    rows = mine.shape[0]
    out[pl.ds(pl.multiple_of(half * rows, rows), rows), :FIRST] = mine[...]
    out[pl.ds(pl.multiple_of((1 - half) * rows, rows), rows), :FIRST] = other[...]
    out[:, FIRST:] = side[...]


def shape(dims, dtype=BF16):
    return jax.ShapeDtypeStruct(dims, dtype)


def far(dims):
    return pltpu.HBM(dims, BF16)


def params():
    return pltpu.CompilerParams(vmem_limit_bytes=40 << 20)


def swap(array, axis):
    return lax.ppermute(array, axis, [(0, 1), (1, 0)])


def shift(array, axis, size, steps):
    return lax.ppermute(array, axis, [(i, (i + steps) % size) for i in range(size)])


def call(kernel, out_shape, *operands, scalars=0, scratch=()):
    many = isinstance(out_shape, list)
    results = pl.pallas_call(
        kernel,
        in_specs=[SM] * scalars + [VM] * (len(operands) - scalars),
        out_specs=[VM] * len(out_shape) if many else VM,
        out_shape=out_shape,
        scratch_shapes=list(scratch),
        compiler_params=params(),
    )(*operands)
    return list(results) if many else results


def compute(tokens, out_grad, gate_weight, up_weight, gate_mask, up_mask):
    width = gate_weight.shape[1]
    count, features = tokens.shape
    half = count // YL
    chunk = half // Z
    rest = features - FIRST
    place = jnp.stack([lax.axis_index(name) for name in ("core", "yl", "x", "yh")])
    copies = pl.pallas_call(
        mask_kernel,
        in_specs=[HB] * 4,
        out_specs=VM,
        out_shape=shape((YH, BLOCK, 2 * width)),
        scratch_shapes=[
            pltpu.SMEM(gate_mask.shape, jnp.int32),
            pltpu.SMEM(up_mask.shape, jnp.int32),
            pltpu.VMEM(gate_weight.shape, BF16),
            pltpu.VMEM(up_weight.shape, BF16),
            pltpu.SemaphoreType.DMA((4,)),
        ],
    )(gate_mask, up_mask, gate_weight, up_weight)
    rows = lax.all_to_all(copies, "yh", 0, 0, tiled=True)
    rows = jnp.broadcast_to(rows[None], (X,) + rows.shape)
    mine = lax.all_to_all(rows, "x", 0, 0, tiled=True)
    other = swap(mine, "core")
    tokens, grad = call(
        prepare_kernel, [shape(tokens.shape), far((count, width))], tokens, out_grad.T
    )
    hidden_t, d_both, send, keep, side = call(
        forward_kernel,
        [
            shape((width, count), F32),
            far((count, 2 * width)),
            far((half, FIRST)),
            far((half, FIRST)),
            far((count, rest)),
        ],
        place,
        tokens,
        grad,
        mine,
        other,
        scalars=1,
        scratch=[pltpu.VMEM((features, 2 * width), BF16)],
    )
    received = swap(send, "yl")
    side = lax.all_to_all(side.reshape(Z, 2 * chunk, rest), "z", 0, 0, tiled=True)
    w_keep, w_send = call(
        weight_kernel,
        [shape((X, YH, BLOCK, 2 * width))] * 2,
        place,
        tokens,
        d_both,
        scalars=1,
    )
    w_received = swap(w_send, "core")
    w_parts = call(pair_kernel, [shape((YH, BLOCK, 2 * width))] * X, w_keep, w_received)
    for steps in range(1, X):
        w_parts[steps] = shift(w_parts[steps], "x", X, steps)
    w_parts = call(rows_kernel, [shape((BLOCK, 2 * width))] * YH, *w_parts)
    for steps in range(1, YH):
        w_parts[steps] = shift(w_parts[steps], "yh", YH, steps)
    grad_gate, grad_up = call(
        final_kernel,
        [shape((BLOCK, width), F32)] * 2,
        gate_mask,
        up_mask,
        *w_parts,
        scalars=2,
    )
    main = call(add_kernel, shape((half, FIRST)), keep, received)
    main = lax.all_to_all(main.reshape(Z, chunk, FIRST), "z", 0, 0, tiled=True)
    side = call(sum_kernel, shape((2 * chunk, rest)), side)
    side_other = swap(side, "yl")
    side = call(add_copies_kernel, shape((Z, 2 * chunk, rest)), side, side_other)
    main = call(sum_copies_kernel, shape((Z, chunk, FIRST)), main)
    main = lax.all_to_all(main, "z", 0, 0, tiled=True).reshape(half, FIRST)
    main_other = swap(main, "yl")
    side = lax.all_to_all(side, "z", 0, 0, tiled=True).reshape(count, rest)
    grad_tokens = call(
        join_kernel, shape((count, features)), place, main, main_other, side, scalars=1
    )
    return (hidden_t.T, grad_tokens, grad_gate, grad_up)


def solution(mesh):
    fine = Mesh(
        np.asarray(mesh.devices).reshape(YH, X, CORE, Z, YL), ("yh", "x", "core", "z", "yl")
    )
    dp = ("yh", "x", "core")
    tensor = ("z", "yl")
    both = P(dp, tensor)
    return jax.shard_map(
        compute,
        mesh=fine,
        in_specs=(P(dp, None), both, both, both, both, both),
        out_specs=(both, P(dp, None), both, both),
        check_vma=False,
    )
```

```python
import jax
import jax.numpy as jnp
import numpy as np
from jax import lax
from jax.experimental import pallas as pl
from jax.experimental.pallas import tpu as pltpu
from jax.sharding import Mesh
from jax.sharding import PartitionSpec as P


BLOCK = 64
BF16 = jnp.bfloat16
F32 = jnp.float32
YH, X, CORE, Z, YL = 4, 4, 2, 8, 2
FIRST = 1664
VM = pl.BlockSpec(memory_space=pltpu.VMEM)
HB = pl.BlockSpec(memory_space=pltpu.HBM)
SM = pl.BlockSpec(memory_space=pltpu.SMEM)


def keep_row(mask_ref, width):
    column = lax.broadcasted_iota(jnp.int32, (1, width), 1) // BLOCK
    keep = jnp.zeros((1, width), F32)
    for block in range(width // BLOCK):
        keep = jnp.where(column == block, mask_ref[0, block].astype(F32), keep)
    return keep


def mask_kernel(gm_hbm, um_hbm, gw_hbm, uw_hbm, out, gm, um, gw, uw, sems):
    moves = [
        pltpu.make_async_copy(source, target, sems.at[index])
        for index, (source, target) in enumerate(
            ((gw_hbm, gw), (uw_hbm, uw), (gm_hbm, gm), (um_hbm, um))
        )
    ]
    for move in moves:
        move.start()
    for move in moves:
        move.wait()
    width = gw.shape[1]
    gate = gw[...].astype(F32) * keep_row(gm, width)
    up = uw[...].astype(F32) * keep_row(um, width)
    both = jnp.concatenate([gate, up], axis=1).astype(BF16)
    for copy in range(YH):
        out[copy] = both


def prepare_kernel(tokens, ogt, tokens_out, grad_out):
    tokens_out[...] = tokens[...]
    grad_out[...] = ogt[...].astype(F32).T


def forward_kernel(place, tokens, grad_ref, *rest):
    mine, other = rest[:X], rest[X : 2 * X]
    hidden_t, d_both, send, keep, side, w = rest[2 * X :]
    core, half, own_x = place[0], place[1], place[2]
    width = grad_ref.shape[1]
    for yh in range(YH):
        for back in range(X):
            x = lax.rem(own_x + (X - back), X)
            row = (yh * X + x) * CORE * BLOCK
            for rows, index in ((mine[back], core), (other[back], 1 - core)):
                start = pl.multiple_of(row + index * BLOCK, BLOCK)
                w[pl.ds(start, BLOCK), :] = rows[yh]
    weights = w[...]
    preact = jnp.dot(tokens[...], weights, preferred_element_type=F32)
    gate = preact[:, :width]
    up = preact[:, width:]
    sigmoid = jax.nn.sigmoid(gate)
    activation = gate * sigmoid
    hidden_t[...] = (activation * up).T
    grad = grad_ref[...]
    d_gate = grad * up * sigmoid * (1.0 + gate * (1.0 - sigmoid))
    d_up = grad * activation
    d_both[...] = jnp.concatenate([d_gate, d_up], axis=1).astype(BF16)
    rows = send.shape[0]
    for out, index in ((send, 1 - half), (keep, half)):
        start = pl.multiple_of(index * rows, rows)
        out[...] = to_tokens(d_both[pl.ds(start, rows), :], weights[:FIRST])
    side[...] = to_tokens(d_both[...], weights[FIRST:])


def to_tokens(grad, weights):
    return lax.dot_general(
        grad, weights, (((1,), (1,)), ((), ())), preferred_element_type=F32
    ).astype(BF16)


def weight_kernel(place, tokens, d_both, keep, send):
    core, own_x, own_yh = place[0], place[2], place[3]
    rows = CORE * BLOCK * 2
    for step in range(YH * X // 2):
        both = lax.dot_general(
            tokens[:, step * rows : (step + 1) * rows],
            d_both[...],
            (((0,), (0,)), ((), ())),
            preferred_element_type=F32,
        ).astype(BF16)
        for pair in range(2):
            yh, x = divmod(step * 2 + pair, X)
            ahead = lax.rem(x + X - own_x, X), lax.rem(yh + YH - own_yh, YH)
            low = both[pair * 128 : pair * 128 + 64]
            high = both[pair * 128 + 64 : pair * 128 + 128]
            first = core == 0
            keep[ahead] = jnp.where(first, low, high)
            send[ahead] = jnp.where(first, high, low)


def final_kernel(gm, um, *refs):
    parts, (grad_gate, grad_up) = refs[:-2], refs[-2:]
    width = grad_gate.shape[1]
    total = parts[0][...].astype(F32)
    for part in parts[1:]:
        total = total + part[...].astype(F32)
    grad_gate[...] = total[:, :width] * keep_row(gm, width)
    grad_up[...] = total[:, width:] * keep_row(um, width)


def pair_kernel(first, second, *outs):
    for index, out in enumerate(outs):
        out[...] = (first[index].astype(F32) + second[index].astype(F32)).astype(BF16)


def rows_kernel(*refs):
    parts, outs = refs[:X], refs[X:]
    for index, out in enumerate(outs):
        total = parts[0][index].astype(F32)
        for part in parts[1:]:
            total = total + part[index].astype(F32)
        out[...] = total.astype(BF16)


def add_kernel(first, second, out):
    out[...] = (first[...].astype(F32) + second[...].astype(F32)).astype(BF16)


def total_of(parts):
    total = parts[0].astype(F32)
    for source in range(1, parts.shape[0]):
        total = total + parts[source].astype(F32)
    return total.astype(BF16)


def sum_kernel(parts, out):
    out[...] = total_of(parts)


def sum_copies_kernel(parts, out):
    total = total_of(parts)
    for copy in range(out.shape[0]):
        out[copy] = total


def add_copies_kernel(first, second, out):
    total = (first[...].astype(F32) + second[...].astype(F32)).astype(BF16)
    for copy in range(out.shape[0]):
        out[copy] = total


def join_main_kernel(place, mine, other, out, sems):
    rows = mine.shape[0]
    moves = []
    for part, index in ((mine, place[1]), (other, 1 - place[1])):
        start = pl.multiple_of(index * rows, rows)
        target = out.at[pl.ds(start, rows), pl.ds(0, FIRST)]
        moves.append(pltpu.make_async_copy(part, target, sems.at[len(moves)]))
    for move in moves:
        move.start()
    for move in moves:
        move.wait()


def join_side_kernel(side, before, out, sem):
    rest = side.shape[1]
    move = pltpu.make_async_copy(side, out.at[:, pl.ds(FIRST, rest)], sem)
    move.start()
    move.wait()


def shape(dims, dtype=BF16):
    return jax.ShapeDtypeStruct(dims, dtype)


def far(dims):
    return pltpu.HBM(dims, BF16)


def params():
    return pltpu.CompilerParams(vmem_limit_bytes=40 << 20)


def swap(array, axis):
    return lax.ppermute(array, axis, [(0, 1), (1, 0)])


def shift(array, axis, size, steps):
    return lax.ppermute(array, axis, [(i, (i + steps) % size) for i in range(size)])


def call(kernel, out_shape, *operands, scalars=0, scratch=()):
    many = isinstance(out_shape, list)
    results = pl.pallas_call(
        kernel,
        in_specs=[SM] * scalars + [VM] * (len(operands) - scalars),
        out_specs=[VM] * len(out_shape) if many else VM,
        out_shape=out_shape,
        scratch_shapes=list(scratch),
        compiler_params=params(),
    )(*operands)
    return list(results) if many else results


def compute(tokens, out_grad, gate_weight, up_weight, gate_mask, up_mask):
    width = gate_weight.shape[1]
    count, features = tokens.shape
    half = count // YL
    chunk = half // Z
    rest = features - FIRST
    place = jnp.stack([lax.axis_index(name) for name in ("core", "yl", "x", "yh")])
    copies = pl.pallas_call(
        mask_kernel,
        in_specs=[HB] * 4,
        out_specs=VM,
        out_shape=shape((YH, BLOCK, 2 * width)),
        scratch_shapes=[
            pltpu.SMEM(gate_mask.shape, jnp.int32),
            pltpu.SMEM(up_mask.shape, jnp.int32),
            pltpu.VMEM(gate_weight.shape, BF16),
            pltpu.VMEM(up_weight.shape, BF16),
            pltpu.SemaphoreType.DMA((4,)),
        ],
    )(gate_mask, up_mask, gate_weight, up_weight)
    rows = lax.all_to_all(copies, "yh", 0, 0, tiled=True)
    mine, other = [rows], []
    for steps in range(1, X):
        mine.append(shift(rows, "x", X, steps))
    for steps in range(X):
        other.append(swap(mine[steps], "core"))
    tokens, grad = call(
        prepare_kernel, [shape(tokens.shape), shape((count, width), F32)], tokens, out_grad.T
    )
    hidden_t, d_both, send, keep, side = call(
        forward_kernel,
        [
            shape((width, count), F32),
            far((count, 2 * width)),
            far((half, FIRST)),
            far((half, FIRST)),
            far((count, rest)),
        ],
        place,
        tokens,
        grad,
        *mine,
        *other,
        scalars=1,
        scratch=[pltpu.VMEM((features, 2 * width), BF16)],
    )
    received = swap(send, "yl")
    side = lax.all_to_all(side.reshape(Z, 2 * chunk, rest), "z", 0, 0, tiled=True)
    w_keep, w_send = call(
        weight_kernel,
        [shape((X, YH, BLOCK, 2 * width))] * 2,
        place,
        tokens,
        d_both,
        scalars=1,
    )
    w_received = swap(w_send, "core")
    w_parts = call(pair_kernel, [shape((YH, BLOCK, 2 * width))] * X, w_keep, w_received)
    for steps in range(1, X):
        w_parts[steps] = shift(w_parts[steps], "x", X, steps)
    w_parts = call(rows_kernel, [shape((BLOCK, 2 * width))] * YH, *w_parts)
    for steps in range(1, YH):
        w_parts[steps] = shift(w_parts[steps], "yh", YH, steps)
    grad_gate, grad_up = call(
        final_kernel,
        [shape((BLOCK, width), F32)] * 2,
        gate_mask,
        up_mask,
        *w_parts,
        scalars=2,
    )
    main = call(add_kernel, shape((half, FIRST)), keep, received)
    main = lax.all_to_all(main.reshape(Z, chunk, FIRST), "z", 0, 0, tiled=True)
    side = call(sum_kernel, shape((2 * chunk, rest)), side)
    side_other = swap(side, "yl")
    side = call(add_copies_kernel, shape((Z, 2 * chunk, rest)), side, side_other)
    main = call(sum_copies_kernel, shape((Z, chunk, FIRST)), main)
    main = lax.all_to_all(main, "z", 0, 0, tiled=True).reshape(half, FIRST)
    main_other = swap(main, "yl")
    side = lax.all_to_all(side, "z", 0, 0, tiled=True).reshape(count, rest)
    grad_tokens = pl.pallas_call(
        join_main_kernel,
        in_specs=[SM, VM, VM],
        out_specs=HB,
        out_shape=far((count, features)),
        scratch_shapes=[pltpu.SemaphoreType.DMA((2,))],
        compiler_params=params(),
    )(place, main, main_other)
    grad_tokens = pl.pallas_call(
        join_side_kernel,
        in_specs=[VM, HB],
        out_specs=HB,
        out_shape=far((count, features)),
        scratch_shapes=[pltpu.SemaphoreType.DMA],
        input_output_aliases={1: 0},
        compiler_params=params(),
    )(side, grad_tokens)
    return (hidden_t.T, grad_tokens, grad_gate, grad_up)


def solution(mesh):
    fine = Mesh(
        np.asarray(mesh.devices).reshape(YH, X, CORE, Z, YL), ("yh", "x", "core", "z", "yl")
    )
    dp = ("yh", "x", "core")
    tensor = ("z", "yl")
    both = P(dp, tensor)
    return jax.shard_map(
        compute,
        mesh=fine,
        in_specs=(P(dp, None), both, both, both, both, both),
        out_specs=(both, P(dp, None), both, both),
        check_vma=False,
    )
```
